256 devices in a mesh: slab: 32 (over y, z), mode: 8 (over x, core).
Axes of the slice: x: 4, y: 4, z: 8, core: 2. Of those that a mesh axis runs over, the one named last changes fastest.
Arguments:
- positions: float32 [3, 524288], P(None, ('slab', 'mode')), may hold values from 0 to 1, as said below
- charges: float32 [524288], P(('slab', 'mode')), may hold values from -0.03125 to 0.03125
- counts: int32 [32], replicated, may hold values from 3840 to 16384, as said below
- box: float32 [2], replicated, may hold values from 0.8 to 1.25
Outputs:
- forces: float32 [3, 524288], P(None, ('slab', 'mode'))
The draws below stay inside these ranges and needn't reach their ends.
Inputs may be any that keep to these rules, and one draw needn't show every extreme that they name: positions[0] and positions[1] are fractional coordinates; positions[2, i] lies strictly between s 0.08 / 32 and (s + 1) 0.08 / 32 for s = i // 16384, and never falls with i within a slab. The live ions of a slab are its first counts[s] slots; some slab is full.
All inputs are finite; a program needn't handle non-finite values.
Results may differ from the reference program's by a relative error of at most 0.0003.
Values sent between devices are 32-bit elements; how exact they have to be, the bound alone decides.
A program may use at most 64 MiB of HBM per device.

```python
import math
import jax
import jax.numpy as jnp
from jax import lax

QDIM = 64
BLOCK = 512
MODES = 4096
ION_SLAB = 16384
IONS = 524288
N_SLAB = 32


slab_span = 0.08


def run_levels(key, run_width, spread):
    step_total = ION_SLAB + 1
    run_count = (step_total + run_width - 1) // run_width
    levels = jnp.exp(jax.random.uniform(key, (N_SLAB, run_count), jnp.float32, -spread, spread))
    run_index = jnp.arange(step_total, dtype=jnp.int32) // run_width
    return levels[:, run_index]


def draw_positions(key, part):
    keys = jax.random.split(jax.random.fold_in(key, 11), 5)
    frac_x = jax.random.uniform(keys[0], (N_SLAB * ION_SLAB,), jnp.float32)
    frac_y = jax.random.uniform(keys[1], (N_SLAB * ION_SLAB,), jnp.float32)
    base_steps = jax.random.uniform(keys[2], (N_SLAB, ION_SLAB + 1), jnp.float32, 0.2, 1.8)
    short_levels = run_levels(keys[3], max(1, BLOCK // 8), 2.0)
    long_levels = run_levels(keys[4], 2 * BLOCK, 4.0)
    steps_up = base_steps * short_levels * long_levels
    running = jnp.cumsum(steps_up, axis=1)
    fraction = running[:, :-1] / running[:, -1:]
    height = slab_span / N_SLAB
    heights = (jnp.arange(N_SLAB, dtype=jnp.float32)[:, None] + 0.001 + 0.998 * fraction) * height
    return jnp.stack([frac_x, frac_y, heights.reshape(-1)]).astype(jnp.float32)


def draw_counts(key, part):
    keys = jax.random.split(jax.random.fold_in(key, 23), 3)
    divisor = jax.random.randint(keys[0], (N_SLAB,), 1, 5)
    jitter = jax.random.randint(keys[1], (N_SLAB,), 0, BLOCK // 2 + 1)
    ragged = ION_SLAB // divisor - jitter
    full_slab = jax.random.randint(keys[2], (), 0, N_SLAB)
    return jnp.where(jnp.arange(N_SLAB) == full_slab, ION_SLAB, ragged).astype(jnp.int32)


def block_scale(rng, dims, shards, smallest, top_value):
    level, own = 1.0, jax.random.fold_in(rng, 6)
    for dim, parts in shards:
        draws = jnp.exp(jax.random.uniform(jax.random.fold_in(own, dim), (parts,), jnp.float32, smallest / len(shards), top_value / len(shards)))
        level = level * jnp.repeat(draws, dims[dim] // parts).reshape([-1 if axis == dim else 1 for axis in range(len(dims))])
    return level


def noise(key, shape, deviation, bound, cuts=(), kind=jnp.bfloat16):
    values = deviation * jax.random.normal(key, shape, jnp.float32)
    if cuts:
        values = values * block_scale(key, shape, cuts, -0.22, 0.18)
    return jnp.clip(values, -bound, bound).astype(kind)


def setup_inputs(seed: int = 0) -> dict:
    seeds = jax.random.split(jax.random.key(seed), 5)
    positions = draw_positions(jax.random.fold_in(seeds[4], 71), 0)
    charges = noise(seeds[1], (IONS,), (0.45 * (IONS * MODES) ** -0.25), 0.03125, ((0, 256),), jnp.float32)
    counts = draw_counts(jax.random.fold_in(seeds[4], 71), 0)
    box = jnp.clip(jnp.exp(jax.random.uniform(seeds[3], (2,), jnp.float32, math.log(0.8), math.log(1.25))), 0.8, 1.25)
    return dict(positions=positions, charges=charges, counts=counts, box=box)


two_pi = 2.0 * math.pi
slab_span = 0.08

def wave_table(first_mode, mode_count, box):
    mode_index = first_mode + jnp.arange(mode_count, dtype=jnp.int32)
    order_p = (mode_index // QDIM + 1).astype(jnp.float32)
    order_q = (mode_index % QDIM - QDIM // 2).astype(jnp.float32)
    wave_x = two_pi * order_p / box[0]
    wave_y = two_pi * order_q / box[1]
    wave_norm = jnp.sqrt(wave_x * wave_x + wave_y * wave_y)
    return (order_p, order_q, wave_x / wave_norm, wave_y / wave_norm, wave_norm)

def phase_terms(mode_info, coords, lower_edge, height):
    order_p, order_q, unit_x, unit_y, wave_norm = mode_info
    phase_angle = two_pi * (order_p[:, None] * coords[0][None, :] + order_q[:, None] * coords[1][None, :])
    ion_depth = coords[2][None, :] - lower_edge
    e_low = jnp.exp(-wave_norm[:, None] * ion_depth)
    e_high = jnp.exp(-wave_norm[:, None] * (height - ion_depth))
    return (jnp.cos(phase_angle), jnp.sin(phase_angle), e_low, e_high)

def force_terms(mode_info, coords, weight, coefficients, lower_edge, height, box):
    order_p, order_q, unit_x, unit_y, wave_norm = mode_info
    cosine, sine_part, e_low, e_high = phase_terms(mode_info, coords, lower_edge, height)
    mode_count, ion_count = cosine.shape
    block_count = coefficients.shape[2]

    def spread(row_values):
        return jnp.broadcast_to(row_values[:, :, None], (mode_count, block_count, BLOCK)).reshape(mode_count, ion_count)
    below_c = e_low * spread(coefficients[0])
    below_s = e_low * spread(coefficients[1])
    above_c = e_high * spread(coefficients[2])
    above_s = e_high * spread(coefficients[3])
    in_plane = sine_part * (below_c + above_c) - cosine * (below_s + above_s)
    normal = cosine * (below_c - above_c) + sine_part * (below_s - above_s)
    scale = 2.0 * two_pi / (box[0] * box[1]) * weight
    return jnp.stack([lax.optimization_barrier(jnp.sum(unit_x[:, None] * in_plane, axis=0)), lax.optimization_barrier(jnp.sum(unit_y[:, None] * in_plane, axis=0)), lax.optimization_barrier(jnp.sum(normal, axis=0))]) * scale[None, :]

def reference(positions, charges, counts, box):
    height = slab_span / N_SLAB
    coords = positions.reshape(3, N_SLAB, ION_SLAB).transpose(1, 0, 2)
    charge = charges.reshape(N_SLAB, ION_SLAB)
    live_mask = jnp.arange(ION_SLAB, dtype=jnp.int32)[None, :] < counts[:, None]
    weight = jnp.where(live_mask, charge, jnp.float32(0.0))
    lower_edges = jnp.arange(N_SLAB, dtype=jnp.int32).astype(jnp.float32) * height
    group_size = 256 if MODES % 256 == 0 else MODES
    first_modes = jnp.arange(MODES // group_size, dtype=jnp.int32) * group_size
    block_count = ION_SLAB // BLOCK

    def slab_moments(slab_item):
        ion_place, ion_weight, lower_edge = slab_item

        def per_group(first_mode):
            mode_info = wave_table(first_mode, group_size, box)
            cosine, sine_part, e_low, e_high = phase_terms(mode_info, ion_place, lower_edge, height)
            upward = ion_weight[None, :] * e_high
            downward = ion_weight[None, :] * e_low
            row_stack = jnp.stack([upward * cosine, upward * sine_part, downward * cosine, downward * sine_part])
            return lax.optimization_barrier(jnp.sum(row_stack.reshape(4, group_size, block_count, BLOCK), axis=3))
        pieces = lax.map(per_group, first_modes)
        return pieces.transpose(1, 0, 2, 3).reshape(4, MODES, block_count)
    moments = lax.map(slab_moments, (coords, weight, lower_edges))
    wave_norm = wave_table(jnp.int32(0), MODES, box)[4]
    decay_step = jnp.exp(-wave_norm * height)
    totals = lax.optimization_barrier(jnp.sum(moments, axis=3))

    def advance(carried, total_here):
        return (decay_step[None, :] * carried + total_here, carried)
    zero_carry = jnp.zeros((2, MODES), jnp.float32)
    _, carry_up = lax.scan(advance, zero_carry, totals[:, 0:2])
    _, carry_down = lax.scan(advance, zero_carry, totals[:, 2:4], reverse=True)
    boost_step = jnp.exp(wave_norm * height)[None, None, :, None]
    prefix_up = jnp.cumsum(moments[:, 0:2], axis=3) - moments[:, 0:2]
    suffix_down = jnp.flip(jnp.cumsum(jnp.flip(moments[:, 2:4], 3), axis=3), 3) - moments[:, 2:4]
    coefficients = jnp.concatenate([carry_up[..., None] + boost_step * prefix_up, carry_down[..., None] + boost_step * suffix_down], axis=1)

    def slab_forces(slab_item):
        ion_place, ion_weight, lower_edge, coeff_table = slab_item

        def per_group(total_force, first_mode):
            mode_info = wave_table(first_mode, group_size, box)
            coeff_part = lax.dynamic_slice_in_dim(coeff_table, first_mode.astype(jnp.int32), group_size, 1)
            return (total_force + force_terms(mode_info, ion_place, ion_weight, coeff_part, lower_edge, height, box), None)
        total_force, _ = lax.scan(per_group, jnp.zeros((3, ION_SLAB), jnp.float32), first_modes)
        return total_force
    forces = lax.map(slab_forces, (coords, weight, lower_edges, coefficients))
    return forces.transpose(1, 0, 2).reshape(3, IONS)
```

```python
import math

import jax
import jax.numpy as jnp
from jax import lax
from jax.experimental import pallas as pl
from jax.experimental.pallas import tpu as pltpu
from jax.sharding import PartitionSpec as P

BLOCK = 512
SLABS = 32
GROUP = 8
OWN = 2048
BLOCKS = OWN // BLOCK
SPAN = 0.08
TWO_PI = 2.0 * math.pi
F32 = jnp.float32
BF16 = jnp.bfloat16

EXP = (
    0.999999988350913, 0.9999999941834263, 0.5000007545561663, 0.16666682366413116,
    0.04165903378572252, 0.008332189708132568, 0.001413565070950797, 0.0002014945763397459,
)
COS = (
    0.9999999890590228, -19.73920449945383, 64.93911745989081, -85.45013953079767,
    60.167630950263465, -25.967599245923743, 6.52865815775625,
)
SIN = (
    6.283185302511503, -41.34170040531721, 81.6051313857832, -76.70301535364747,
    42.02592698447418, -14.899846663536497, 3.2381375046186873,
)
POWERS = 8

LOW = 64 * POWERS
EXTRA = LOW + 64 * 3
ROWS = EXTRA + 64


def horner(coefs, z):
    acc = coefs[-1] * z + coefs[-2]
    for c in coefs[-3::-1]:
        acc = acc * z + c
    return acc


def frac(t):
    return t - jnp.round(t)


def cos_turn(r):
    return horner(COS, r * r)


def sin_turn(r):
    return r * horner(SIN, r * r)


def iota(shape, dim):
    return lax.broadcasted_iota(jnp.int32, shape, dim)


def split(v):
    hi = v.astype(BF16)
    return hi, (v - hi.astype(F32)).astype(BF16)


def y_order(index):
    order = jnp.where(index < 32, index, jnp.where(index == 32, 32, index - 32))
    return order.astype(F32)


def waves(order_p, order_q, box0, box1):
    wave_x = TWO_PI * order_p / box0
    wave_y = TWO_PI * order_q / box1
    return wave_x, wave_y, jnp.sqrt(wave_x * wave_x + wave_y * wave_y)


def turn(row):
    return pltpu.roll(row, 64, 1)


def kernel(
    counts, box, pos, chg, out,
    tf, e_ref, we, stack, tab, tab32, up, down, total, rx1, sums, rx2, tx3, base, pre, suf, table, weights,
    send1, recv1, send2, recv2, send3, recv3,
):
    s = lax.axis_index("slab")
    r = lax.axis_index("mode")
    barrier = pltpu.get_barrier_semaphore()

    def greet_mode(o, _):
        pl.semaphore_signal(barrier, 1, device_id={"mode": lax.rem(r + o, GROUP)})
        return 0

    def greet_slab(o, _):
        pl.semaphore_signal(barrier, 1, device_id={"slab": lax.rem(s + o, SLABS)})
        return 0

    lax.fori_loop(1, GROUP, greet_mode, 0)
    lax.fori_loop(1, SLABS, greet_slab, 0)

    box0, box1 = box[0], box[1]
    height = SPAN / SLABS
    lower = s.astype(F32) * height

    lane = iota((64, 128), 1)
    row = iota((64, 128), 0)
    order_p = (lane % 64 + 1).astype(F32)
    _, _, norm = waves(order_p, y_order(row), box0, box1)
    half = norm * (0.5 * height)
    decay = jnp.exp(-half)
    boost = jnp.exp(norm * height)
    power = decay
    for l in range(POWERS):
        tab[l] = power * EXP[l]
        power = power * half
    lane1 = iota((8, 128), 1)
    row1 = iota((8, 128), 0)
    p1 = (lane1 % 64 + 1).astype(F32)
    _, _, norm32 = waves(p1, jnp.full((8, 128), 32.0, F32), box0, box1)
    half32 = norm32 * (0.5 * height)
    power = jnp.exp(-half32)
    t32 = jnp.zeros((8, 128), F32)
    for l in range(POWERS):
        t32 = jnp.where(row1 == l, power * EXP[l], t32)
        power = power * half32
    tab32[...] = t32

    live = counts[s] - r * OWN
    slot = iota((1, OWN), 1)
    weights[...] = jnp.where(slot < live, chg[...], 0.0)
    sign = jnp.where(iota((1, 128), 1) < 64, -1.0, 1.0)

    def moments(b, _):
        ds = pl.ds(pl.multiple_of(b * BLOCK, BLOCK), BLOCK)
        x = pos[0:1, ds]
        y = pos[1:2, ds]
        w = weights[0:1, ds]
        u = (pos[2:3, ds] - lower) * (2.0 / height) - 1.0
        for g in range(4):
            p = (iota((16, BLOCK), 0) + (16 * g + 1)).astype(F32)
            t = frac(p * x)
            for half_row, v in ((0, cos_turn(t)), (64, sin_turn(t))):
                at = half_row + 16 * g
                e_ref[at : at + 16, ds] = v
                hi, lo = split(w * v)
                we[at : at + 16, :] = hi
                we[128 + at : 144 + at, :] = lo
        powers = [jnp.ones_like(u)]
        for l in range(1, POWERS):
            powers.append(powers[-1] * u)
        for g in range(4):
            t = frac(y_order(iota((16, BLOCK), 0) + 16 * g) * y)
            f = cos_turn(t) if g < 2 else sin_turn(t)
            for l in range(POWERS):
                at = 64 * l + 16 * g
                v = f * powers[l] if l else f
                if l < 3:
                    hi, lo = split(v)
                    tf[LOW + at : LOW + at + 16, ds] = lo
                else:
                    hi = v.astype(BF16)
                tf[at : at + 16, ds] = hi
        c32 = cos_turn(frac(32.0 * y))
        v = jnp.concatenate([c32 * q for q in powers], axis=0)
        hi = v.astype(BF16).astype(F32)
        tf[EXTRA : EXTRA + 16, ds] = jnp.concatenate([hi, hi], axis=0).astype(BF16)
        tf[EXTRA + 16 : EXTRA + 32, ds] = jnp.concatenate([v - hi, jnp.zeros_like(v)], axis=0).astype(BF16)
        tf[EXTRA + 32 : EXTRA + 64, ds] = jnp.zeros((32, BLOCK), BF16)

        stack[...] = lax.dot_general(
            tf[:, ds], we[...], (((1,), (1,)), ((), ())), preferred_element_type=F32
        )
        sides = []
        for first in (0, 1):
            acc = None
            acc32 = None
            for l in range(first, POWERS, 2):
                m = stack[64 * l : 64 * l + 64, 0:128] + stack[64 * l : 64 * l + 64, 128:256]
                if l < 3:
                    m = m + stack[LOW + 64 * l : LOW + 64 * l + 64, 0:128]
                acc = tab[l] * m if acc is None else acc + tab[l] * m
            sides.append(acc)
        m32 = stack[EXTRA : EXTRA + 8, 0:128] + stack[EXTRA : EXTRA + 8, 128:256] + stack[EXTRA + 16 : EXTRA + 24, 0:128]
        m32 = tab32[...] * m32
        even = jnp.sum(jnp.where(row1 % 2 == 0, m32, 0.0), axis=0, keepdims=True)
        odd = jnp.sum(jnp.where(row1 % 2 == 1, m32, 0.0), axis=0, keepdims=True)
        for ref, m, m_last in (
            (up, sides[0] + sides[1], even + odd),
            (down, sides[0] - sides[1], even - odd),
        ):
            fixed = 0.5 * (m[32:33] + sign * turn(m_last))
            ref[b] = jnp.where(row == 32, fixed, m)
        return 0

    lax.fori_loop(0, BLOCKS, moments, 0)

    sum_up = up[0]
    for b in range(1, BLOCKS):
        sum_up = sum_up + up[b]
    sum_down = down[0]
    for b in range(1, BLOCKS):
        sum_down = sum_down + down[b]
    total[:, 0] = sum_up.reshape(GROUP, 8, 128)
    total[:, 1] = sum_down.reshape(GROUP, 8, 128)
    rx1[r] = total[r]

    pl.semaphore_wait(barrier, GROUP - 1 + SLABS - 1)

    def copy1(j):
        return pltpu.make_async_remote_copy(
            total.at[j], rx1.at[r], send1.at[j], recv1.at[r], device_id={"mode": j}
        )

    def take1(j):
        return pltpu.make_async_remote_copy(
            total.at[j], rx1.at[j], send1.at[j], recv1.at[j], device_id={"mode": j}
        )

    def over_group(act):
        def step(o, _):
            act(lax.rem(r + o, GROUP))
            return 0

        lax.fori_loop(1, GROUP, step, 0)

    def over_slabs(act):
        def step(o, _):
            act(lax.rem(s + o, SLABS))
            return 0

        lax.fori_loop(1, SLABS, step, 0)

    over_group(lambda j: copy1(j).start())

    run = jnp.zeros((64, 128), F32)
    for b in range(BLOCKS):
        pre[b] = boost * run
        run = run + up[b]
    run = jnp.zeros((64, 128), F32)
    for b in range(BLOCKS - 1, -1, -1):
        suf[b] = boost * run
        run = run + down[b]

    over_group(lambda j: take1(j).wait())

    slab_up = rx1[0, 0]
    slab_down = rx1[0, 1]
    for j in range(1, GROUP):
        slab_up = slab_up + rx1[j, 0]
        slab_down = slab_down + rx1[j, 1]
    sums[0] = slab_up
    sums[1] = slab_down
    rx2[s] = jnp.zeros((8, 128), F32)

    def copy2(t, slot_at):
        return pltpu.make_async_remote_copy(
            sums.at[jnp.where(t < s, 1, 0)], rx2.at[slot_at], send2.at[t], recv2.at[slot_at], device_id={"slab": t}
        )

    over_slabs(lambda t: copy2(t, s).start())

    lane2 = iota((128, 128), 1)
    p2 = (iota((128, 128), 0) % 64 + 1).astype(F32)
    q2 = y_order(lane2 % 64)
    kx, ky, norm2 = waves(p2, q2, box0, box1)
    half2 = norm2 * (0.5 * height)
    scale = 2.0 * TWO_PI / (box0 * box1)
    common = scale * jnp.where(q2 == 0.0, 1.0, 2.0) * jnp.exp(-half2)
    square = half2 * half2
    odd_lane = lane2 >= 64
    power = jnp.where(odd_lane, half2, 1.0) * common
    ux = kx / norm2
    uy = ky / norm2
    for j in range(POWERS // 2):
        t = power * jnp.where(odd_lane, EXP[2 * j + 1], EXP[2 * j])
        table[0, j] = t * ux
        table[1, j] = t * uy
        table[2, j] = -t
        power = power * square
    kx32, ky32, _ = waves(p1, jnp.full((8, 128), 32.0, F32), box0, box1)
    base32 = (2.0 * scale) * t32
    x32 = base32 * (kx32 / norm32)
    y32 = -base32 * (ky32 / norm32)

    slice_row = 8 * r + row1
    _, _, norm_s = waves(p1, y_order(slice_row), box0, box1)
    step_s = norm_s * height
    boost_s = jnp.exp(step_s)
    run = jnp.zeros((8, 128), F32)
    for j in range(GROUP):
        tx3[j, 0] = boost_s * run
        run = run + rx1[j, 0]
    run = jnp.zeros((8, 128), F32)
    for j in range(GROUP - 1, -1, -1):
        tx3[j, 1] = boost_s * run
        run = run + rx1[j, 1]

    over_slabs(lambda t: copy2(t, t).wait())

    carry_up = jnp.zeros((8, 128), F32)
    carry_down = jnp.zeros((8, 128), F32)
    for t in range(SLABS):
        gap = jnp.maximum(jnp.abs(s - t) - 1, 0).astype(F32)
        term = jnp.exp(-step_s * gap) * rx2[t]
        carry_up = carry_up + jnp.where(t < s, term, 0.0)
        carry_down = carry_down + jnp.where(t > s, term, 0.0)
    for j in range(GROUP):
        tx3[j, 0] = tx3[j, 0] + carry_up
        tx3[j, 1] = tx3[j, 1] + carry_down
    base[r] = tx3[r]

    def copy3(j, slot_at):
        return pltpu.make_async_remote_copy(
            tx3.at[j], base.at[slot_at], send3.at[j], recv3.at[slot_at], device_id={"mode": j}
        )

    over_group(lambda j: copy3(j, r).start())
    over_group(lambda j: copy3(j, j).wait())

    parity = row1 % 2 == 0
    zeros8 = jnp.zeros((8, 128), F32)

    def forces(b, _):
        ds = pl.ds(pl.multiple_of(b * BLOCK, BLOCK), BLOCK)
        g_up = base[:, 0].reshape(64, 128) + pre[b]
        g_down = base[:, 1].reshape(64, 128) + suf[b]
        plus = g_up + g_down
        minus = g_down - g_up
        plus32 = -sign * turn(plus[32:33])
        minus32 = -sign * turn(minus[32:33])

        def swapped(g, g32):
            return jnp.where(row == 32, g32, jnp.concatenate([-g[32:64], g[0:32]], axis=0))

        straight = jnp.concatenate([plus, minus], axis=0).T
        crossed = jnp.concatenate([swapped(plus, plus32), swapped(minus, minus32)], axis=0).T
        sources = (straight, crossed, turn(straight))
        extras = (
            x32 * jnp.where(parity, plus32, minus32),
            y32 * jnp.where(parity, plus[32:33], minus[32:33]),
            -base32 * jnp.where(parity, minus32, plus32),
        )
        main_rows = []
        low_rows = []
        for f in range(3):
            his = []
            los = []
            for j in range(POWERS // 2):
                h = table[f, j] * sources[f]
                if j < 2:
                    hi, lo = split(h)
                    los.append(lo)
                else:
                    hi = h.astype(BF16)
                his.append(hi)
            v = extras[f]
            hi8 = v.astype(BF16).astype(F32)
            spread = jnp.concatenate(
                [jnp.zeros((64, 128), F32), hi8, v - hi8, hi8, jnp.zeros((40, 128), F32)], axis=0
            ).T
            last = jnp.where(lane2 < 64, table[f, 1] * sources[f], spread).astype(BF16)
            main_rows.append(jnp.concatenate(his + [his[0], last], axis=1))
            low_rows.append(jnp.concatenate(los, axis=1))
        mains = jnp.concatenate(main_rows, axis=0)
        lows = jnp.concatenate(low_rows, axis=0)
        product = lax.dot_general(mains, tf[:, ds], (((1,), (0,)), ((), ())), preferred_element_type=F32)
        product = product + lax.dot_general(
            lows, tf[0:256, ds], (((1,), (0,)), ((), ())), preferred_element_type=F32
        )
        w = weights[0:1, ds]
        cosine = e_ref[0:64, ds]
        sine = e_ref[64:128, ds]
        fx = jnp.sum(sine * product[0:64] - cosine * product[64:128], axis=0, keepdims=True)
        fy = jnp.sum(cosine * product[128:192] + sine * product[192:256], axis=0, keepdims=True)
        fz = jnp.sum(cosine * product[256:320] + sine * product[320:384], axis=0, keepdims=True)
        out[0:1, ds] = w * fx
        out[1:2, ds] = w * fy
        out[2:3, ds] = w * fz
        return 0

    lax.fori_loop(0, BLOCKS, forces, 0)


def shards(positions, charges, counts, box):
    vmem = pl.BlockSpec(memory_space=pltpu.VMEM)
    smem = pl.BlockSpec(memory_space=pltpu.SMEM)
    tile = (8, 128)
    return pl.pallas_call(
        kernel,
        out_shape=jax.ShapeDtypeStruct((3, OWN), F32),
        in_specs=[smem, smem, vmem, vmem],
        out_specs=vmem,
        scratch_shapes=[
            pltpu.VMEM((ROWS, OWN), BF16),
            pltpu.VMEM((128, OWN), F32),
            pltpu.VMEM((256, BLOCK), BF16),
            pltpu.VMEM((ROWS, 256), F32),
            pltpu.VMEM((POWERS, 64, 128), F32),
            pltpu.VMEM(tile, F32),
            pltpu.VMEM((BLOCKS, 64, 128), F32),
            pltpu.VMEM((BLOCKS, 64, 128), F32),
            pltpu.VMEM((GROUP, 2) + tile, F32),
            pltpu.VMEM((GROUP, 2) + tile, F32),
            pltpu.VMEM((2,) + tile, F32),
            pltpu.VMEM((SLABS,) + tile, F32),
            pltpu.VMEM((GROUP, 2) + tile, F32),
            pltpu.VMEM((GROUP, 2) + tile, F32),
            pltpu.VMEM((BLOCKS, 64, 128), F32),
            pltpu.VMEM((BLOCKS, 64, 128), F32),
            pltpu.VMEM((3, POWERS // 2, 128, 128), F32),
            pltpu.VMEM((1, OWN), F32),
            pltpu.SemaphoreType.DMA((GROUP,)),
            pltpu.SemaphoreType.DMA((GROUP,)),
            pltpu.SemaphoreType.DMA((SLABS,)),
            pltpu.SemaphoreType.DMA((SLABS,)),
            pltpu.SemaphoreType.DMA((GROUP,)),
            pltpu.SemaphoreType.DMA((GROUP,)),
        ],
        compiler_params=pltpu.CompilerParams(collective_id=0, has_side_effects=True),
    )(counts, box, positions, charges.reshape(1, OWN))


def solution(mesh):
    return jax.shard_map(
        shards,
        mesh=mesh,
        in_specs=(P(None, ("slab", "mode")), P(("slab", "mode")), P(), P()),
        out_specs=P(None, ("slab", "mode")),
        check_vma=False,
    )
```

```python
import math

import jax
import jax.numpy as jnp
from jax import lax
from jax.experimental import pallas as pl
from jax.experimental.pallas import tpu as pltpu
from jax.sharding import PartitionSpec as P

BLOCK = 512
SLABS = 32
GROUP = 8
OWN = 2048
BLOCKS = OWN // BLOCK
SPAN = 0.08
TWO_PI = 2.0 * math.pi
F32 = jnp.float32
BF16 = jnp.bfloat16

EXP = (
    0.999999988350913, 0.9999999941834263, 0.5000007545561663, 0.16666682366413116,
    0.04165903378572252, 0.008332189708132568, 0.001413565070950797, 0.0002014945763397459,
)
COS = (
    0.9999999890590228, -19.73920449945383, 64.93911745989081, -85.45013953079767,
    60.167630950263465, -25.967599245923743, 6.52865815775625,
)
SIN = (
    6.283185302511503, -41.34170040531721, 81.6051313857832, -76.70301535364747,
    42.02592698447418, -14.899846663536497, 3.2381375046186873,
)
POWERS = 8

LOW = 64 * POWERS
EXTRA = LOW + 64 * 3
ROWS = EXTRA + 64


def horner(coefs, z):
    acc = coefs[-1] * z + coefs[-2]
    for c in coefs[-3::-1]:
        acc = acc * z + c
    return acc


def frac(t):
    return t - jnp.round(t)


def cos_turn(r):
    return horner(COS, r * r)


def sin_turn(r):
    return r * horner(SIN, r * r)


def iota(shape, dim):
    return lax.broadcasted_iota(jnp.int32, shape, dim)


def split(v):
    hi = v.astype(BF16)
    return hi, (v - hi.astype(F32)).astype(BF16)


def y_order(index):
    order = jnp.where(index < 32, index, jnp.where(index == 32, 32, index - 32))
    return order.astype(F32)


def waves(order_p, order_q, box0, box1):
    wave_x = TWO_PI * order_p / box0
    wave_y = TWO_PI * order_q / box1
    return wave_x, wave_y, jnp.sqrt(wave_x * wave_x + wave_y * wave_y)


def turn(row):
    return pltpu.roll(row, 64, 1)


def hop_key(offset, size):
    return min(offset, size - offset)


GROUP_OFFSETS = sorted(
    ((dx, dc) for dx in range(4) for dc in range(2) if dx or dc), key=lambda o: -(2 * hop_key(o[0], 4) + o[1])
)
SLAB_OFFSETS = sorted(
    ((dy, dz) for dy in range(4) for dz in range(8) if dy or dz), key=lambda o: -(hop_key(o[0], 4) + hop_key(o[1], 8))
)


def kernel(
    counts_h, box_h, pos_h, chg_h, out,
    counts, box, pos, chg,
    tf, e_ref, we, stack, tab, up, down, total, rx1, sums, rx2, tx3, base, pre, suf, table, weights, decays, ht, part,
    load, ready, send1, recv1, send2, recv2, send3, recv3,
):
    s = lax.axis_index("slab")
    r = lax.axis_index("mode")
    at_y, at_z = s // 8, s % 8
    at_x, core = r // 2, r % 2

    def mate(offset):
        return lax.rem(at_x + offset[0], 4) * 2 + lax.rem(core + offset[1], 2)

    def slab_at(offset):
        return lax.rem(at_y + offset[0], 4) * 8 + lax.rem(at_z + offset[1], 8)

    barrier = pltpu.get_barrier_semaphore()
    lines = [o for o in SLAB_OFFSETS if o[0] == 0 or o[1] == 0]
    y_line = [o for o in SLAB_OFFSETS if o[1] == 0]
    for o in lines:
        pl.semaphore_signal(barrier, 1, device_id={"slab": slab_at(o)})
    for o in GROUP_OFFSETS:
        pl.semaphore_signal(barrier, 1, device_id={"mode": mate(o)})
    loads = [
        pltpu.make_async_copy(src, dst, load.at[i])
        for i, (src, dst) in enumerate(((pos_h, pos), (chg_h, chg), (counts_h, counts), (box_h, box)))
    ]
    for c in loads:
        c.start()
    height = SPAN / SLABS
    lower = s.astype(F32) * height
    lane = iota((64, 128), 1)
    row = iota((64, 128), 0)
    lane1 = iota((8, 128), 1)
    row1 = iota((8, 128), 0)
    p1 = (lane1 % 64 + 1).astype(F32)
    sign = jnp.where(iota((1, 128), 1) < 64, -1.0, 1.0)
    for c in loads:
        c.wait()
    box0, box1 = box[0], box[1]

    order_p = (lane % 64 + 1).astype(F32)
    _, _, norm = waves(order_p, y_order(row), box0, box1)
    half = norm * (0.5 * height)
    power = jnp.exp(-half)
    for l in range(POWERS):
        tab[l] = power * EXP[l]
        power = power * half
    _, _, norm32 = waves(p1, jnp.full((8, 128), 32.0, F32), box0, box1)
    half32 = norm32 * (0.5 * height)
    power = jnp.exp(-half32)
    t32 = jnp.zeros((8, 128), F32)
    for l in range(POWERS):
        t32 = jnp.where(row1 == l, power * EXP[l], t32)
        power = power * half32

    live = counts[s] - r * OWN
    slot = iota((1, OWN), 1)
    weights[...] = jnp.where(slot < live, chg[...], 0.0)

    def functions(b):
        ds = pl.ds(b * BLOCK, BLOCK)
        x = pos[0:1, ds]
        y = pos[1:2, ds]
        w = weights[0:1, ds]
        u = (pos[2:3, ds] - lower) * (2.0 / height) - 1.0
        for g in range(4):
            p = (iota((16, BLOCK), 0) + (16 * g + 1)).astype(F32)
            t = frac(p * x)
            for half_row, v in ((0, cos_turn(t)), (64, sin_turn(t))):
                at = half_row + 16 * g
                e_ref[at : at + 16, ds] = v
                hi, lo = split(w * v)
                we[b % 2, at : at + 16, :] = hi
                we[b % 2, 128 + at : 144 + at, :] = lo
        powers = [jnp.ones_like(u)]
        for l in range(1, POWERS):
            powers.append(powers[-1] * u)
        for g in range(4):
            t = frac(y_order(iota((16, BLOCK), 0) + 16 * g) * y)
            f = cos_turn(t) if g < 2 else sin_turn(t)
            for l in range(POWERS):
                at = 64 * l + 16 * g
                v = f * powers[l] if l else f
                if l < 3:
                    hi, lo = split(v)
                    tf[LOW + at : LOW + at + 16, ds] = lo
                else:
                    hi = v.astype(BF16)
                tf[at : at + 16, ds] = hi
        c32 = cos_turn(frac(32.0 * y))
        v = jnp.concatenate([c32 * q for q in powers], axis=0)
        hi = v.astype(BF16).astype(F32)
        tf[EXTRA : EXTRA + 16, ds] = jnp.concatenate([hi, hi], axis=0).astype(BF16)
        tf[EXTRA + 16 : EXTRA + 32, ds] = jnp.concatenate([v - hi, jnp.zeros_like(v)], axis=0).astype(BF16)
        tf[EXTRA + 32 : EXTRA + 64, ds] = jnp.zeros((32, BLOCK), BF16)

    def products(b):
        stack[b % 2] = lax.dot_general(
            tf[:, pl.ds(b * BLOCK, BLOCK)], we[b % 2], (((1,), (1,)), ((), ())), preferred_element_type=F32
        )

    def moments(b):
        m_of = stack.at[b % 2]
        sides = []
        for first in (0, 1):
            acc = None
            for l in range(first, POWERS, 2):
                m = m_of[64 * l : 64 * l + 64, 0:128] + m_of[64 * l : 64 * l + 64, 128:256]
                if l < 3:
                    m = m + m_of[LOW + 64 * l : LOW + 64 * l + 64, 0:128]
                acc = tab[l] * m if acc is None else acc + tab[l] * m
            sides.append(acc)
        m32 = m_of[EXTRA : EXTRA + 8, 0:128] + m_of[EXTRA : EXTRA + 8, 128:256] + m_of[EXTRA + 16 : EXTRA + 24, 0:128]
        m32 = t32 * m32
        even = jnp.sum(jnp.where(row1 % 2 == 0, m32, 0.0), axis=0, keepdims=True)
        odd = jnp.sum(jnp.where(row1 % 2 == 1, m32, 0.0), axis=0, keepdims=True)
        for ref, m, m_last in (
            (up, sides[0] + sides[1], even + odd),
            (down, sides[0] - sides[1], even - odd),
        ):
            fixed = 0.5 * (m[32:33] + sign * turn(m_last))
            ref[b] = jnp.where(row == 32, fixed, m)

    for b in range(BLOCKS):
        functions(b)
        products(b)
        moments(b)

    for side, ref in enumerate((up, down)):
        whole = (ref[0] + ref[1]) + (ref[2] + ref[3])
        total[:, side] = whole.reshape(GROUP, 8, 128)

    pl.semaphore_wait(barrier, len(lines) + len(GROUP_OFFSETS))
    for o in GROUP_OFFSETS:
        j = mate(o)
        pltpu.make_async_remote_copy(total.at[j], rx1.at[r], send1, recv1, device_id={"mode": j}).start()
    for o in y_line:
        pl.semaphore_signal(ready, 1, device_id={"slab": slab_at(o)})
    rx1[r] = total[r]

    boost = jnp.exp(norm * height)
    run = jnp.zeros((64, 128), F32)
    for b in range(BLOCKS):
        pre[b] = boost * run
        run = run + up[b]
    run = jnp.zeros((64, 128), F32)
    for b in range(BLOCKS - 1, -1, -1):
        suf[b] = boost * run
        run = run + down[b]

    lane2 = iota((128, 128), 1)
    p2 = (iota((128, 128), 0) % 64 + 1).astype(F32)
    q2 = y_order(lane2 % 64)
    kx, ky, norm2 = waves(p2, q2, box0, box1)
    half2 = norm2 * (0.5 * height)
    scale = 2.0 * TWO_PI / (box0 * box1)
    common = scale * jnp.where(q2 == 0.0, 1.0, 2.0) * jnp.exp(-half2)
    square = half2 * half2
    odd_lane = lane2 >= 64
    power = jnp.where(odd_lane, half2, 1.0) * common
    ux = kx / norm2
    uy = ky / norm2
    for j in range(POWERS // 2):
        t = power * jnp.where(odd_lane, EXP[2 * j + 1], EXP[2 * j])
        table[0, j] = t * ux
        table[1, j] = t * uy
        table[2, j] = -t
        power = power * square
    kx32, ky32, _ = waves(p1, jnp.full((8, 128), 32.0, F32), box0, box1)
    base32 = (2.0 * scale) * t32
    x32 = base32 * (kx32 / norm32)
    y32 = -base32 * (ky32 / norm32)
    parity = row1 % 2 == 0

    _, _, norm_s = waves(p1, y_order(8 * r + row1), box0, box1)
    step_s = norm_s * height
    boost_s = jnp.exp(step_s)
    for t in range(SLABS):
        gap = jnp.maximum(jnp.abs(s - t) - 1, 0).astype(F32)
        term = jnp.exp(-step_s * gap)
        decays[0, t] = jnp.where(t < s, term, 0.0)
        decays[1, t] = jnp.where(t > s, term, 0.0)
    rx2[s] = jnp.zeros((8, 128), F32)

    def weave(g_up, g_down):
        plus = g_up + g_down
        minus = g_down - g_up
        plus32 = -sign * turn(plus[32:33])
        minus32 = -sign * turn(minus[32:33])

        def swapped(g, g32):
            return jnp.where(row == 32, g32, jnp.concatenate([-g[32:64], g[0:32]], axis=0))

        straight = jnp.concatenate([plus, minus], axis=0).T
        crossed = jnp.concatenate([swapped(plus, plus32), swapped(minus, minus32)], axis=0).T
        sources = (straight, crossed, turn(straight))
        extras = (
            x32 * jnp.where(parity, plus32, minus32),
            y32 * jnp.where(parity, plus[32:33], minus[32:33]),
            -base32 * jnp.where(parity, minus32, plus32),
        )
        for f in range(3):
            rows = pl.ds(128 * f, 128)
            for j in range(POWERS // 2):
                h = table[f, j] * sources[f]
                if j < 2:
                    hi, lo = split(h)
                    ht[rows, 768 + 128 * j : 896 + 128 * j] = lo
                else:
                    hi = h.astype(BF16)
                ht[rows, 128 * j : 128 * j + 128] = hi
                if j == 0:
                    ht[rows, 512:640] = hi
            v = extras[f]
            hi8 = v.astype(BF16).astype(F32)
            spread = jnp.concatenate(
                [jnp.zeros((64, 128), F32), hi8, v - hi8, hi8, jnp.zeros((40, 128), F32)], axis=0
            ).T
            ht[rows, 640:768] = jnp.where(lane2 < 64, table[f, 1] * sources[f], spread).astype(BF16)

    def pull(b):
        ds = pl.ds(b * BLOCK, BLOCK)
        product = lax.dot_general(
            ht[:, 0:768], tf[:, ds], (((1,), (0,)), ((), ())), preferred_element_type=F32
        ) + lax.dot_general(
            ht[:, 768:1024], tf[0:256, ds], (((1,), (0,)), ((), ())), preferred_element_type=F32
        )
        cosine = e_ref[0:64, ds]
        sine = e_ref[64:128, ds]
        fx = jnp.sum(sine * product[0:64] - cosine * product[64:128], axis=0, keepdims=True)
        fy = jnp.sum(cosine * product[128:192] + sine * product[192:256], axis=0, keepdims=True)
        fz = jnp.sum(cosine * product[256:320] + sine * product[320:384], axis=0, keepdims=True)
        return jnp.concatenate([fx, fy, fz], axis=0)

    def local(b):
        weave(pre[b], suf[b])
        part[:, pl.ds(b * BLOCK, BLOCK)] = pull(b)

    local(0)
    local(1)

    pltpu.make_async_copy(rx1.at[0:7], rx1.at[0:7], recv1).wait()

    slab_up = rx1[0, 0]
    slab_down = rx1[0, 1]
    for j in range(1, GROUP):
        slab_up = slab_up + rx1[j, 0]
        slab_down = slab_down + rx1[j, 1]
    sums[0] = slab_up
    sums[1] = slab_down

    pl.semaphore_wait(ready, len(y_line))
    for o in SLAB_OFFSETS:
        t = slab_at(o)
        pltpu.make_async_remote_copy(
            sums.at[jnp.where(t < s, 1, 0)], rx2.at[s], send2, recv2, device_id={"slab": t}
        ).start()

    run = jnp.zeros((8, 128), F32)
    for j in range(GROUP):
        tx3[j, 0] = boost_s * run
        run = run + rx1[j, 0]
    run = jnp.zeros((8, 128), F32)
    for j in range(GROUP - 1, -1, -1):
        tx3[j, 1] = boost_s * run
        run = run + rx1[j, 1]
    local(2)
    local(3)

    pltpu.make_async_copy(rx2.at[0:31], rx2.at[0:31], recv2).wait()

    for side in range(2):
        terms = [decays[side, t] * rx2[t] for t in range(SLABS)]
        while len(terms) > 1:
            terms = [terms[i] + terms[i + 1] for i in range(0, len(terms), 2)]
        for j in range(GROUP):
            tx3[j, side] = tx3[j, side] + terms[0]

    for o in GROUP_OFFSETS:
        j = mate(o)
        pltpu.make_async_remote_copy(tx3.at[j], base.at[r], send3, recv3, device_id={"mode": j}).start()
    base[r] = tx3[r]
    pltpu.make_async_copy(base.at[0:7], base.at[0:7], recv3).wait()

    weave(base[:, 0].reshape(64, 128), base[:, 1].reshape(64, 128))
    for b in range(BLOCKS):
        ds = pl.ds(b * BLOCK, BLOCK)
        out[:, ds] = weights[0:1, ds] * (part[:, ds] + pull(b))

    pltpu.make_async_copy(total.at[0:7], total.at[0:7], send1).wait()
    pltpu.make_async_copy(rx2.at[0:31], rx2.at[0:31], send2).wait()
    pltpu.make_async_copy(tx3.at[0:7], tx3.at[0:7], send3).wait()


def shards(positions, charges, counts, box):
    vmem = pl.BlockSpec(memory_space=pltpu.VMEM)
    anywhere = pl.BlockSpec(memory_space=pl.ANY)
    tile = (8, 128)
    return pl.pallas_call(
        kernel,
        out_shape=jax.ShapeDtypeStruct((3, OWN), F32),
        in_specs=[anywhere] * 4,
        out_specs=vmem,
        scratch_shapes=[
            pltpu.SMEM((SLABS,), jnp.int32),
            pltpu.SMEM((2,), F32),
            pltpu.VMEM((3, OWN), F32),
            pltpu.VMEM((1, OWN), F32),
            pltpu.VMEM((ROWS, OWN), BF16),
            pltpu.VMEM((128, OWN), F32),
            pltpu.VMEM((2, 256, BLOCK), BF16),
            pltpu.VMEM((2, ROWS, 256), F32),
            pltpu.VMEM((POWERS, 64, 128), F32),
            pltpu.VMEM((BLOCKS, 64, 128), F32),
            pltpu.VMEM((BLOCKS, 64, 128), F32),
            pltpu.VMEM((GROUP, 2) + tile, F32),
            pltpu.VMEM((GROUP, 2) + tile, F32),
            pltpu.VMEM((2,) + tile, F32),
            pltpu.VMEM((SLABS,) + tile, F32),
            pltpu.VMEM((GROUP, 2) + tile, F32),
            pltpu.VMEM((GROUP, 2) + tile, F32),
            pltpu.VMEM((BLOCKS, 64, 128), F32),
            pltpu.VMEM((BLOCKS, 64, 128), F32),
            pltpu.VMEM((3, POWERS // 2, 128, 128), F32),
            pltpu.VMEM((1, OWN), F32),
            pltpu.VMEM((2, SLABS) + tile, F32),
            pltpu.VMEM((384, 1024), BF16),
            pltpu.VMEM((3, OWN), F32),
            pltpu.SemaphoreType.DMA((4,)),
            pltpu.SemaphoreType.REGULAR,
            pltpu.SemaphoreType.DMA,
            pltpu.SemaphoreType.DMA,
            pltpu.SemaphoreType.DMA,
            pltpu.SemaphoreType.DMA,
            pltpu.SemaphoreType.DMA,
            pltpu.SemaphoreType.DMA,
        ],
        compiler_params=pltpu.CompilerParams(collective_id=0, has_side_effects=True),
    )(counts, box, positions, charges.reshape(1, OWN))


def solution(mesh):
    return jax.shard_map(
        shards,
        mesh=mesh,
        in_specs=(P(None, ("slab", "mode")), P(("slab", "mode")), P(), P()),
        out_specs=P(None, ("slab", "mode")),
        check_vma=False,
    )
```

```python
import math

import jax
import jax.numpy as jnp
from jax import lax
from jax.experimental import pallas as pl
from jax.experimental.pallas import tpu as pltpu
from jax.sharding import PartitionSpec as P

BLOCK = 512
SLABS = 32
GROUP = 8
OWN = 2048
BLOCKS = OWN // BLOCK
SPAN = 0.08
TWO_PI = 2.0 * math.pi
F32 = jnp.float32
BF16 = jnp.bfloat16

EXP = (
    0.999999988350913, 0.9999999941834263, 0.5000007545561663, 0.16666682366413116,
    0.04165903378572252, 0.008332189708132568, 0.001413565070950797, 0.0002014945763397459,
)
COS = (
    0.9999999890590228, -19.73920449945383, 64.93911745989081, -85.45013953079767,
    60.167630950263465, -25.967599245923743, 6.52865815775625,
)
SIN = (
    6.283185302511503, -41.34170040531721, 81.6051313857832, -76.70301535364747,
    42.02592698447418, -14.899846663536497, 3.2381375046186873,
)
POWERS = 8

LOW = 64 * POWERS
EXTRA = LOW + 64 * 3
ROWS = EXTRA + 64


def horner(coefs, z):
    acc = coefs[-1] * z + coefs[-2]
    for c in coefs[-3::-1]:
        acc = acc * z + c
    return acc


def frac(t):
    return t - jnp.round(t)


def cos_turn(r):
    return horner(COS, r * r)


def sin_turn(r):
    return r * horner(SIN, r * r)


def iota(shape, dim):
    return lax.broadcasted_iota(jnp.int32, shape, dim)


def split(v):
    hi = v.astype(BF16)
    return hi, (v - hi.astype(F32)).astype(BF16)


def y_order(index):
    order = jnp.where(index < 32, index, jnp.where(index == 32, 32, index - 32))
    return order.astype(F32)


def waves(order_p, order_q, box0, box1):
    wave_x = TWO_PI * order_p / box0
    wave_y = TWO_PI * order_q / box1
    return wave_x, wave_y, jnp.sqrt(wave_x * wave_x + wave_y * wave_y)


def turn(row):
    return pltpu.roll(row, 64, 1)


def hop_key(offset, size):
    return min(offset, size - offset)


GROUP_OFFSETS = sorted(
    ((dx, dc) for dx in range(4) for dc in range(2) if dx or dc), key=lambda o: -(2 * hop_key(o[0], 4) + o[1])
)
SLAB_OFFSETS = sorted(
    ((dy, dz) for dy in range(4) for dz in range(8) if dy or dz), key=lambda o: -(hop_key(o[0], 4) + hop_key(o[1], 8))
)


def kernel(
    counts_h, box_h, pos_h, chg_h, out,
    counts, box, pos, chg,
    tf, e_ref, we, stack, tab, up, down, total, rx1, sums, rx2, tx3, base, pre, suf, table, weights, decays, ht, part,
    load, ready, send1, recv1, send2, recv2, send3, recv3,
):
    s = lax.axis_index("slab")
    r = lax.axis_index("mode")
    at_y, at_z = s // 8, s % 8
    at_x, core = r // 2, r % 2

    def mate(offset):
        return lax.rem(at_x + offset[0], 4) * 2 + lax.rem(core + offset[1], 2)

    def slab_at(offset):
        return lax.rem(at_y + offset[0], 4) * 8 + lax.rem(at_z + offset[1], 8)

    barrier = pltpu.get_barrier_semaphore()
    lines = [o for o in SLAB_OFFSETS if o[0] == 0 or o[1] == 0]
    y_line = [o for o in SLAB_OFFSETS if o[1] == 0]
    for o in lines:
        pl.semaphore_signal(barrier, 1, device_id={"slab": slab_at(o)})
    for o in GROUP_OFFSETS:
        pl.semaphore_signal(barrier, 1, device_id={"mode": mate(o)})
    loads = [
        pltpu.make_async_copy(src, dst, load.at[i])
        for i, (src, dst) in enumerate(((pos_h, pos), (chg_h, chg), (counts_h, counts), (box_h, box)))
    ]
    for c in loads:
        c.start()
    height = SPAN / SLABS
    lower = s.astype(F32) * height
    lane = iota((64, 128), 1)
    row = iota((64, 128), 0)
    lane1 = iota((8, 128), 1)
    row1 = iota((8, 128), 0)
    p1 = (lane1 % 64 + 1).astype(F32)
    sign = jnp.where(iota((1, 128), 1) < 64, -1.0, 1.0)
    for c in loads:
        c.wait()
    box0, box1 = box[0], box[1]

    order_p = (lane % 64 + 1).astype(F32)
    _, _, norm = waves(order_p, y_order(row), box0, box1)
    half = norm * (0.5 * height)
    power = jnp.exp(-half)
    for l in range(POWERS):
        tab[l] = power * EXP[l]
        power = power * half
    _, _, norm32 = waves(p1, jnp.full((8, 128), 32.0, F32), box0, box1)
    half32 = norm32 * (0.5 * height)
    power = jnp.exp(-half32)
    t32 = jnp.zeros((8, 128), F32)
    for l in range(POWERS):
        t32 = jnp.where(row1 == l, power * EXP[l], t32)
        power = power * half32

    live = counts[s] - r * OWN
    slot = iota((1, OWN), 1)
    weights[...] = jnp.where(slot < live, chg[...], 0.0)

    def functions(b):
        ds = pl.ds(b * BLOCK, BLOCK)
        x = pos[0:1, ds]
        y = pos[1:2, ds]
        w = weights[0:1, ds]
        u = (pos[2:3, ds] - lower) * (2.0 / height) - 1.0
        for g in range(4):
            p = (iota((16, BLOCK), 0) + (16 * g + 1)).astype(F32)
            t = frac(p * x)
            for half_row, v in ((0, cos_turn(t)), (64, sin_turn(t))):
                at = half_row + 16 * g
                e_ref[at : at + 16, ds] = v
                hi, lo = split(w * v)
                we[b % 2, at : at + 16, :] = hi
                we[b % 2, 128 + at : 144 + at, :] = lo
        powers = [jnp.ones_like(u)]
        for l in range(1, POWERS):
            powers.append(powers[-1] * u)
        for g in range(4):
            t = frac(y_order(iota((16, BLOCK), 0) + 16 * g) * y)
            f = cos_turn(t) if g < 2 else sin_turn(t)
            for l in range(POWERS):
                at = 64 * l + 16 * g
                v = f * powers[l] if l else f
                if l < 3:
                    hi, lo = split(v)
                    tf[LOW + at : LOW + at + 16, ds] = lo
                else:
                    hi = v.astype(BF16)
                tf[at : at + 16, ds] = hi
        c32 = cos_turn(frac(32.0 * y))
        v = jnp.concatenate([c32 * q for q in powers], axis=0)
        hi = v.astype(BF16).astype(F32)
        tf[EXTRA : EXTRA + 16, ds] = jnp.concatenate([hi, hi], axis=0).astype(BF16)
        tf[EXTRA + 16 : EXTRA + 32, ds] = jnp.concatenate([v - hi, jnp.zeros_like(v)], axis=0).astype(BF16)
        tf[EXTRA + 32 : EXTRA + 64, ds] = jnp.zeros((32, BLOCK), BF16)

    def products(b):
        stack[b % 2] = lax.dot_general(
            tf[:, pl.ds(b * BLOCK, BLOCK)], we[b % 2], (((1,), (1,)), ((), ())), preferred_element_type=F32
        )

    def moments(b):
        m_of = stack.at[b % 2]
        sides = []
        for first in (0, 1):
            acc = None
            for l in range(first, POWERS, 2):
                m = m_of[64 * l : 64 * l + 64, 0:128] + m_of[64 * l : 64 * l + 64, 128:256]
                if l < 3:
                    m = m + m_of[LOW + 64 * l : LOW + 64 * l + 64, 0:128]
                acc = tab[l] * m if acc is None else acc + tab[l] * m
            sides.append(acc)
        m32 = m_of[EXTRA : EXTRA + 8, 0:128] + m_of[EXTRA : EXTRA + 8, 128:256] + m_of[EXTRA + 16 : EXTRA + 24, 0:128]
        m32 = t32 * m32
        even = jnp.sum(jnp.where(row1 % 2 == 0, m32, 0.0), axis=0, keepdims=True)
        odd = jnp.sum(jnp.where(row1 % 2 == 1, m32, 0.0), axis=0, keepdims=True)
        for ref, m, m_last in (
            (up, sides[0] + sides[1], even + odd),
            (down, sides[0] - sides[1], even - odd),
        ):
            fixed = 0.5 * (m[32:33] + sign * turn(m_last))
            ref[b] = jnp.where(row == 32, fixed, m)

    for b in range(BLOCKS):
        functions(b)
        products(b)
        moments(b)

    for side, ref in enumerate((up, down)):
        whole = (ref[0] + ref[1]) + (ref[2] + ref[3])
        total[:, side] = whole.reshape(GROUP, 8, 128)

    pl.semaphore_wait(barrier, len(lines) + len(GROUP_OFFSETS))
    for o in GROUP_OFFSETS:
        j = mate(o)
        pltpu.make_async_remote_copy(total.at[j], rx1.at[r], send1, recv1, device_id={"mode": j}).start()
    for o in y_line:
        pl.semaphore_signal(ready, 1, device_id={"slab": slab_at(o)})
    rx1[r] = total[r]

    boost = jnp.exp(norm * height)
    run = jnp.zeros((64, 128), F32)
    for b in range(BLOCKS):
        pre[b] = boost * run
        run = run + up[b]
    run = jnp.zeros((64, 128), F32)
    for b in range(BLOCKS - 1, -1, -1):
        suf[b] = boost * run
        run = run + down[b]

    lane2 = iota((128, 128), 1)
    p2 = (iota((128, 128), 0) % 64 + 1).astype(F32)
    q2 = y_order(lane2 % 64)
    kx, ky, norm2 = waves(p2, q2, box0, box1)
    half2 = norm2 * (0.5 * height)
    scale = 2.0 * TWO_PI / (box0 * box1)
    common = scale * jnp.where(q2 == 0.0, 1.0, 2.0) * jnp.exp(-half2)
    square = half2 * half2
    odd_lane = lane2 >= 64
    power = jnp.where(odd_lane, half2, 1.0) * common
    ux = kx / norm2
    uy = ky / norm2
    for j in range(POWERS // 2):
        t = power * jnp.where(odd_lane, EXP[2 * j + 1], EXP[2 * j])
        table[0, j] = t * ux
        table[1, j] = t * uy
        table[2, j] = -t
        power = power * square
    kx32, ky32, _ = waves(p1, jnp.full((8, 128), 32.0, F32), box0, box1)
    base32 = (2.0 * scale) * t32
    x32 = base32 * (kx32 / norm32)
    y32 = -base32 * (ky32 / norm32)
    parity = row1 % 2 == 0

    _, _, norm_s = waves(p1, y_order(8 * r + row1), box0, box1)
    step_s = norm_s * height
    boost_s = jnp.exp(step_s)
    for t in range(SLABS):
        gap = jnp.maximum(jnp.abs(s - t) - 1, 0).astype(F32)
        term = jnp.exp(-step_s * gap)
        decays[0, t] = jnp.where(t < s, term, 0.0)
        decays[1, t] = jnp.where(t > s, term, 0.0)
    rx2[s] = jnp.zeros((8, 128), F32)

    def weave(g_up, g_down):
        plus = g_up + g_down
        minus = g_down - g_up
        plus32 = -sign * turn(plus[32:33])
        minus32 = -sign * turn(minus[32:33])

        def swapped(g, g32):
            return jnp.where(row == 32, g32, jnp.concatenate([-g[32:64], g[0:32]], axis=0))

        straight = jnp.concatenate([plus, minus], axis=0).T
        crossed = jnp.concatenate([swapped(plus, plus32), swapped(minus, minus32)], axis=0).T
        sources = (straight, crossed, turn(straight))
        extras = (
            x32 * jnp.where(parity, plus32, minus32),
            y32 * jnp.where(parity, plus[32:33], minus[32:33]),
            -base32 * jnp.where(parity, minus32, plus32),
        )
        for f in range(3):
            rows = pl.ds(128 * f, 128)
            for j in range(POWERS // 2):
                h = table[f, j] * sources[f]
                if j < 2:
                    hi, lo = split(h)
                    ht[rows, 768 + 128 * j : 896 + 128 * j] = lo
                else:
                    hi = h.astype(BF16)
                ht[rows, 128 * j : 128 * j + 128] = hi
                if j == 0:
                    ht[rows, 512:640] = hi
            v = extras[f]
            hi8 = v.astype(BF16).astype(F32)
            spread = jnp.concatenate(
                [jnp.zeros((64, 128), F32), hi8, v - hi8, hi8, jnp.zeros((40, 128), F32)], axis=0
            ).T
            ht[rows, 640:768] = jnp.where(lane2 < 64, table[f, 1] * sources[f], spread).astype(BF16)

    def pull(b):
        ds = pl.ds(b * BLOCK, BLOCK)
        product = lax.dot_general(
            ht[:, 0:768], tf[:, ds], (((1,), (0,)), ((), ())), preferred_element_type=F32
        ) + lax.dot_general(
            ht[:, 768:1024], tf[0:256, ds], (((1,), (0,)), ((), ())), preferred_element_type=F32
        )
        cosine = e_ref[0:64, ds]
        sine = e_ref[64:128, ds]
        fx = jnp.sum(sine * product[0:64] - cosine * product[64:128], axis=0, keepdims=True)
        fy = jnp.sum(cosine * product[128:192] + sine * product[192:256], axis=0, keepdims=True)
        fz = jnp.sum(cosine * product[256:320] + sine * product[320:384], axis=0, keepdims=True)
        return jnp.concatenate([fx, fy, fz], axis=0)

    def local(b):
        weave(pre[b], suf[b])
        part[:, pl.ds(b * BLOCK, BLOCK)] = pull(b)

    local(0)
    local(1)

    pltpu.make_async_copy(rx1.at[0:7], rx1.at[0:7], recv1).wait()

    slab_up = rx1[0, 0]
    slab_down = rx1[0, 1]
    for j in range(1, GROUP):
        slab_up = slab_up + rx1[j, 0]
        slab_down = slab_down + rx1[j, 1]
    sums[0] = slab_up
    sums[1] = slab_down

    pl.semaphore_wait(ready, len(y_line))
    for o in SLAB_OFFSETS:
        t = slab_at(o)
        pltpu.make_async_remote_copy(
            sums.at[jnp.where(t < s, 1, 0)], rx2.at[s], send2, recv2, device_id={"slab": t}
        ).start()

    run = jnp.zeros((8, 128), F32)
    for j in range(GROUP):
        tx3[j, 0] = boost_s * run
        run = run + rx1[j, 0]
    run = jnp.zeros((8, 128), F32)
    for j in range(GROUP - 1, -1, -1):
        tx3[j, 1] = boost_s * run
        run = run + rx1[j, 1]
    local(2)
    local(3)

    pltpu.make_async_copy(rx2.at[0:31], rx2.at[0:31], recv2).wait()

    for side in range(2):
        terms = [decays[side, t] * rx2[t] for t in range(SLABS)]
        while len(terms) > 1:
            terms = [terms[i] + terms[i + 1] for i in range(0, len(terms), 2)]
        for j in range(GROUP):
            tx3[j, side] = tx3[j, side] + terms[0]

    for o in GROUP_OFFSETS:
        j = mate(o)
        pltpu.make_async_remote_copy(tx3.at[j], base.at[r], send3, recv3, device_id={"mode": j}).start()
    base[r] = tx3[r]
    pltpu.make_async_copy(base.at[0:7], base.at[0:7], recv3).wait()

    weave(base[:, 0].reshape(64, 128), base[:, 1].reshape(64, 128))
    for b in range(BLOCKS):
        ds = pl.ds(b * BLOCK, BLOCK)
        out[:, ds] = weights[0:1, ds] * (part[:, ds] + pull(b))

    pltpu.make_async_copy(total.at[0:7], total.at[0:7], send1).wait()
    pltpu.make_async_copy(rx2.at[0:31], rx2.at[0:31], send2).wait()
    pltpu.make_async_copy(tx3.at[0:7], tx3.at[0:7], send3).wait()


def shards(positions, charges, counts, box):
    vmem = pl.BlockSpec(memory_space=pltpu.VMEM)
    anywhere = pl.BlockSpec(memory_space=pl.ANY)
    tile = (8, 128)
    return pl.pallas_call(
        kernel,
        out_shape=pltpu.VMEM((3, OWN), F32),
        in_specs=[anywhere] * 4,
        out_specs=vmem,
        scratch_shapes=[
            pltpu.SMEM((SLABS,), jnp.int32),
            pltpu.SMEM((2,), F32),
            pltpu.VMEM((3, OWN), F32),
            pltpu.VMEM((1, OWN), F32),
            pltpu.VMEM((ROWS, OWN), BF16),
            pltpu.VMEM((128, OWN), F32),
            pltpu.VMEM((2, 256, BLOCK), BF16),
            pltpu.VMEM((2, ROWS, 256), F32),
            pltpu.VMEM((POWERS, 64, 128), F32),
            pltpu.VMEM((BLOCKS, 64, 128), F32),
            pltpu.VMEM((BLOCKS, 64, 128), F32),
            pltpu.VMEM((GROUP, 2) + tile, F32),
            pltpu.VMEM((GROUP, 2) + tile, F32),
            pltpu.VMEM((2,) + tile, F32),
            pltpu.VMEM((SLABS,) + tile, F32),
            pltpu.VMEM((GROUP, 2) + tile, F32),
            pltpu.VMEM((GROUP, 2) + tile, F32),
            pltpu.VMEM((BLOCKS, 64, 128), F32),
            pltpu.VMEM((BLOCKS, 64, 128), F32),
            pltpu.VMEM((3, POWERS // 2, 128, 128), F32),
            pltpu.VMEM((1, OWN), F32),
            pltpu.VMEM((2, SLABS) + tile, F32),
            pltpu.VMEM((384, 1024), BF16),
            pltpu.VMEM((3, OWN), F32),
            pltpu.SemaphoreType.DMA((4,)),
            pltpu.SemaphoreType.REGULAR,
            pltpu.SemaphoreType.DMA,
            pltpu.SemaphoreType.DMA,
            pltpu.SemaphoreType.DMA,
            pltpu.SemaphoreType.DMA,
            pltpu.SemaphoreType.DMA,
            pltpu.SemaphoreType.DMA,
        ],
        compiler_params=pltpu.CompilerParams(collective_id=0, has_side_effects=True),
    )(counts, box, positions, charges.reshape(1, OWN))


def solution(mesh):
    return jax.shard_map(
        shards,
        mesh=mesh,
        in_specs=(P(None, ("slab", "mode")), P(("slab", "mode")), P(), P()),
        out_specs=P(None, ("slab", "mode")),
        check_vma=False,
    )
```
